256 devices in a mesh: group: 4 (over y), expert: 64 (over z, x, core).
Axes of the slice: x: 4, y: 4, z: 8, core: 2. Of those that a mesh axis runs over, the one named last changes fastest.
Arguments:
- tokens: bfloat16 [1024, 7168], P(('group', 'expert')), may hold values from -6 to 6
- expert_ids: int32 [1024, 8], P(('group', 'expert')), may hold values from 0 to 31, all different within a row; in each aligned block of 4 rows (0 to 3, 4 to 7, ...) at most 2 rows name the same one
- gate_weights: bfloat16 [1024, 8], P(('group', 'expert')), may hold values from 0.049804688 to 0.5
- w_gate: bfloat16 [256, 7168, 256], P(('group', 'expert')), may hold values from -0.0625 to 0.0625
- w_up: bfloat16 [256, 7168, 256], P(('group', 'expert')), may hold values from -0.0625 to 0.0625
- w_down: bfloat16 [256, 256, 7168], P(('group', 'expert')), may hold values from -0.125 to 0.125
Outputs:
- mixed: bfloat16 [1024, 7168], P(('group', 'expert'))
The draws below stay inside these ranges and needn't reach their ends.
Inputs may be any that keep to these rules, and one draw needn't show every extreme that they name: `expert_ids`: each row names 8 different experts. Among the 4 rows of one device no expert is named by more than 2 rows, and in some device some expert is named by exactly 2 rows.
All inputs are finite; a program needn't handle non-finite values.
Results may differ from the reference program's by a relative error of at most 0.014.
Values may be sent and summed in bfloat16 or wider, within the bound.
A program may use at most 128 MiB of HBM per device.

```python
import math
import jax
import jax.numpy as jnp
import numpy as np
from jax import lax

D = 7168
FF = 2048
TOP = 8
EXP_GRP = 8
ROWS = 4
CAP = 2
EXPERTS = 32
SPLIT = 8
FF_SHARD = 256
TOKENS = 1024
N_GROUP = 4
N_EXPERT = 64


def block_scale(rng, dims, cuts, least, largest):
    def one(position, blocks):
        heights = jax.random.uniform(jax.random.fold_in(jax.random.fold_in(rng, 6), position), (blocks,), jnp.float32, least / len(cuts), largest / len(cuts))
        return jnp.repeat(jnp.exp(heights), dims[position] // blocks).reshape((-1,) + (1,) * (len(dims) - position - 1))

    factor_of = one(*cuts[0])
    for cut in cuts[1:]:
        factor_of = factor_of * one(*cut)
    return factor_of


def shared_out(own_key, own, number, rows, amount, top, reach, slope):
    sequence = jax.random.permutation(own_key, amount)
    heavy_load, ordinary = load_shares(amount, rows * top, reach, slope, True), load_shares(amount, rows * top, reach, slope, False)
    places = jnp.arange(amount)

    def named(tallies, offset_by):
        used = int((tallies > 0).sum())
        fixed = max(1, used // 4)
        moved = fixed + (places - fixed + offset_by * (used - fixed)) % max(1, amount - fixed)
        return jnp.zeros((amount,), jnp.int32).at[sequence[jnp.where(places < fixed, places, moved)]].set(jnp.asarray(tallies, jnp.int32))

    tallies = jnp.where(number % 4 == 0, named(heavy_load, number // 4), named(ordinary, number - number // 4 - 1))
    mixed = jax.random.permutation(jax.random.fold_in(own, 3), amount)
    giver, sink = mixed[0:amount // 2 * 2:2], mixed[1:amount // 2 * 2:2]
    room = jnp.minimum(tallies[giver] - 1, reach - tallies[sink]) // 2
    room = jnp.where((giver == sequence[0]) | (sink == sequence[0]) | (tallies[sink] == 0), 0, jnp.maximum(room, 0))
    moved = jax.random.randint(jax.random.fold_in(own, 4), (amount // 2,), 0, 1 << 20) % (room + 1)
    tallies = tallies.at[giver].add(-moved).at[sink].add(moved)
    items = jnp.searchsorted(jnp.cumsum(tallies), jnp.arange(rows * top), side="right").astype(jnp.int32)
    grid = items.reshape(top, rows).T
    grid = grid[jax.random.permutation(jax.random.fold_in(own, 1), rows)]
    offset_by = jax.random.randint(jax.random.fold_in(own, 2), (rows, 1), 0, top)
    return jnp.take_along_axis(grid, (jnp.arange(top)[None, :] + offset_by) % top, axis=1)


def load_shares(amount, total, reach, slope, full):
    loads = [(1 << 20) // math.isqrt(rank ** slope) + 1 for rank in range(1, amount + 1)]
    largest = reach if full else min(reach, max(-(-total // amount), total * loads[0] // sum(loads)))
    least = 1 if total - largest >= amount - 1 else 0
    counts, spare = [largest] + [least] * (amount - 1), total - largest - least * (amount - 1)
    while spare > 0:
        free = [i for i in range(1, amount) if counts[i] < largest] or [i for i in range(1, amount) if counts[i] < reach]
        pool, budget = sum([loads[i] for i in free]), spare
        for i in free:
            extra = min(reach - counts[i], max(1, budget * loads[i] // pool), spare)
            counts[i] = counts[i] + extra
            spare = spare - extra
    return np.array(counts)


def centred(key, dims, spread, bound, cuts=(), held_as=jnp.bfloat16):
    result = spread * jax.random.normal(key, dims, jnp.float32)
    if cuts:
        result = result * block_scale(key, dims, cuts, -0.22, 0.18)
    return jnp.clip(result, -bound, bound).astype(held_as)


def setup_inputs(seed: int = 0) -> dict:
    key_of = jax.random.split(jax.random.key(seed), 7)
    tokens = centred(key_of[0], (TOKENS, D), 1.0, 6.0, ((0, 256),))
    expert_ids_keys = jax.random.split(jax.random.fold_in(key_of[1], 1), TOKENS // ROWS)
    expert_ids_turns = jax.random.permutation(jax.random.fold_in(key_of[1], 3), TOKENS // ROWS)
    expert_ids = jax.vmap(lambda own, number: shared_out(jax.random.fold_in(key_of[1], 2), own, number, ROWS, EXPERTS, TOP, CAP, 2))(expert_ids_keys, expert_ids_turns).reshape((TOKENS, TOP))
    gate_weights = jnp.clip(jnp.exp(math.log(0.5) - 2.306499 * jax.random.uniform(key_of[2], (TOKENS, TOP), jnp.float32) ** block_scale(key_of[2], (TOKENS, TOP), ((0, 256),), -0.2, 0.2)), 0.049804688, 0.5).astype(jnp.bfloat16)
    w_gate = centred(key_of[3], (EXPERTS * SPLIT, D, FF_SHARD), D ** -0.5, 0.0625, ((0, 256),))
    w_up = centred(key_of[4], (EXPERTS * SPLIT, D, FF_SHARD), D ** -0.5, 0.0625, ((0, 256),))
    w_down = centred(key_of[5], (EXPERTS * SPLIT, FF_SHARD, D), FF ** -0.5, 0.125, ((0, 256),))
    return {"tokens": tokens, "expert_ids": expert_ids, "gate_weights": gate_weights, "w_gate": w_gate, "w_up": w_up, "w_down": w_down}


def reference(tokens, expert_ids, gate_weights, w_gate, w_up, w_down):
    experts = N_GROUP * EXP_GRP
    split = N_EXPERT // EXP_GRP
    total = tokens.shape[0]
    width = tokens.shape[1]
    labels = jnp.arange(experts, dtype=jnp.int32)
    match = expert_ids[:, :, None] == labels[None, None, :]
    named = jnp.any(match, axis=1)
    weight = jnp.sum(jnp.where(match, gate_weights.astype(jnp.float32)[:, :, None], jnp.float32(0.0)), axis=1)
    most = N_GROUP * N_EXPERT * CAP

    def one_expert(carry, index):
        column = named[:, index]
        picked = jnp.nonzero(column, size=most, fill_value=0)[0].astype(jnp.int32)
        valid = jnp.arange(most, dtype=jnp.int32) < jnp.sum(column.astype(jnp.int32))
        rows = tokens[picked]
        start = (index * split).astype(jnp.int32)
        gate_rows = lax.dynamic_slice_in_dim(w_gate, start, split, 0)
        up_rows = lax.dynamic_slice_in_dim(w_up, start, split, 0)
        down_rows = lax.dynamic_slice_in_dim(w_down, start, split, 0)
        gate_full = jnp.transpose(gate_rows, (1, 0, 2)).reshape(width, -1)
        up_full = jnp.transpose(up_rows, (1, 0, 2)).reshape(width, -1)
        gate_val = jnp.dot(rows, gate_full, preferred_element_type=jnp.float32)
        up_val = jnp.dot(rows, up_full, preferred_element_type=jnp.float32)
        hidden = (jax.nn.silu(gate_val) * up_val).astype(jnp.bfloat16)
        hidden = hidden.reshape(most, split, -1)
        parts = jnp.einsum("msf,sfd->msd", hidden.astype(jnp.float32), down_rows.astype(jnp.float32),
                           precision=lax.Precision.HIGHEST).astype(jnp.bfloat16)
        expert_out = jnp.sum(parts.astype(jnp.float32), axis=1).astype(jnp.bfloat16)
        scale = jnp.where(valid, weight[picked, index], jnp.float32(0.0))
        carry = carry.at[picked].add(scale[:, None] * expert_out.astype(jnp.float32))
        return carry, None

    summed, _ = lax.scan(one_expert, jnp.zeros((total, width), jnp.float32), labels)
    return summed.astype(jnp.bfloat16)
```

```python
import functools

import jax
import jax.numpy as jnp
from jax import lax
from jax.experimental import pallas as pl
from jax.experimental.pallas import tpu as pltpu
from jax.sharding import PartitionSpec as P

EXP_GRP = 8
CAP = 2
CORES = 2
WIDTH = 1024
MESH = pl.DeviceIdType.MESH
F32 = jnp.float32
BF16 = jnp.bfloat16


def routing_table(ids, gates, experts):
    rows, top = ids.shape
    lane = lax.broadcasted_iota(jnp.int32, (rows, 128), 1)
    named = jnp.zeros((rows, 128), F32)
    weight = jnp.zeros((rows, 128), F32)
    for k in range(top):
        chosen = ids[:, k : k + 1]
        named = jnp.where(lane == chosen, F32(1.0), named)
        weight = jnp.where(lane == chosen + experts, gates[:, k : k + 1], weight)
    earlier = jnp.zeros((1, 128), F32)
    out = []
    for row in range(rows):
        mine = named[row : row + 1]
        out.append(mine * (F32(1.0) + earlier) + weight[row : row + 1])
        earlier = earlier + mine
    return out


def kernel(
    groups, zs, xs, rows, chunks,
    tok_ref, ids_ref, gates_ref, gate_hbm, up_hbm, down_hbm, out_ref,
    w_gate, w_up, w_down, zbuf, meta, rowbuf, sel, mix, ysend, arrived,
    acc_gate, acc_up, hidden, psend, pair, part, keep_b, keep_own,
    send_far, send_f, send_b, got_far, got_f, got_b, vsend, vbuf, msend, fbuf,
    w_sem, meta_sem, z_sem, y_sem, b_sem, f_sem, fwd_sem, core_sem,
    pair_sem, far_sem, rf_sem, rb_sem, v_sem, fin_sem, send_sem,
):
    y = lax.axis_index("group")
    member = lax.axis_index("expert")
    z = member // (xs * CORES)
    x = (member // CORES) % xs
    c = member % CORES
    other = 1 - c
    step = 1 - 2 * c
    xf = (x + step + xs) % xs
    xb = (x - step + xs) % xs
    far = (x + 2) % xs
    experts = groups * EXP_GRP
    slots = zs * CAP

    def at(y_, z_, x_, c_):
        return (y_, (z_ * xs + x_) * CORES + c_)

    z_peers = [(z + d) % zs for d in range(1, zs)]
    y_peers = [(y + d) % groups for d in range(1, groups)]

    def send(src, dst, which, recv, where):
        pltpu.make_async_remote_copy(
            src_ref=src, dst_ref=dst, send_sem=send_sem.at[which], recv_sem=recv,
            device_id=where, device_id_type=MESH,
        ).start()

    def wait(ref, sem):
        pltpu.make_async_copy(ref, ref, sem).wait()

    weights = [
        pltpu.make_async_copy(gate_hbm.at[0], w_gate, w_sem.at[0]),
        pltpu.make_async_copy(up_hbm.at[0], w_up, w_sem.at[1]),
    ]
    for copy in weights:
        copy.start()
    for k in range(chunks):
        pltpu.make_async_copy(
            down_hbm.at[0, :, pl.ds(k * WIDTH, WIDTH)], w_down.at[k], w_sem.at[2]
        ).start()

    barrier = pltpu.get_barrier_semaphore()
    partners = (
        [at(y, p, x, c) for p in z_peers]
        + [at(p, z, x, c) for p in y_peers]
        + [at(y, z, xf, c), at(y, z, xb, c), at(y, z, x, other)]
    )
    for p in partners:
        pl.semaphore_signal(barrier, inc=1, device_id=p, device_id_type=MESH)

    table = routing_table(ids_ref[...], gates_ref[...].astype(F32), experts)
    for row in range(rows):
        meta[z, row : row + 1, :] = table[row]
    for k in range(chunks):
        zbuf[k, z] = tok_ref[:, k * WIDTH : (k + 1) * WIDTH]
    acc_gate[...] = jnp.zeros_like(acc_gate)
    acc_up[...] = jnp.zeros_like(acc_up)
    pl.semaphore_wait(barrier, len(partners))

    for p in z_peers:
        send(meta.at[z], meta.at[z], 0, meta_sem, at(y, p, x, c))

    def send_tokens(k):
        for p in z_peers:
            send(zbuf.at[k, z], zbuf.at[k, z], 1, z_sem.at[k], at(y, p, x, c))

    send_tokens(0)
    if chunks > 1:
        send_tokens(1)

    wait(meta.at[pl.ds(0, zs - 1)], meta_sem)
    for p in range(zs):
        rowbuf[rows * p : rows * (p + 1), 0:128] = meta[p]
    line = rowbuf[:, 0:128]
    total = zs * rows
    lane = lax.broadcasted_iota(jnp.int32, (total, 128), 1)
    row_id = lax.broadcasted_iota(jnp.int32, (total, groups * slots), 0)
    col_id = lax.broadcasted_iota(jnp.int32, (total, groups * slots), 1)
    same = (row_id // rows) == ((col_id % slots) // CAP)
    place = (col_id % CAP + 1).astype(F32)
    pick = jnp.zeros((total, groups * slots), F32)
    blend = jnp.zeros((total, groups * slots), F32)
    for q in range(groups):
        expert = q * EXP_GRP + z
        code = jnp.sum(jnp.where(lane == expert, line, F32(0.0)), axis=1, keepdims=True)
        weight = jnp.sum(jnp.where(lane == expert + experts, line, F32(0.0)), axis=1, keepdims=True)
        hit = same & (col_id // slots == q) & (code == place)
        pick = jnp.where(hit, F32(1.0), pick)
        blend = jnp.where(hit, weight, blend)
    mix[...] = blend.astype(BF16)
    n = groups * slots
    eye = (
        lax.broadcasted_iota(jnp.int32, (n, n), 0) == lax.broadcasted_iota(jnp.int32, (n, n), 1)
    ).astype(F32).astype(BF16)
    sel[...] = lax.dot_general(
        eye, pick.astype(BF16), (((1,), (1,)), ((), ())), preferred_element_type=F32
    ).astype(BF16)

    def dispatch(t, carry):
        @pl.when(t < chunks)
        def _():
            k = t
            wait(zbuf.at[k, pl.ds(0, zs - 1)], z_sem.at[k])
            for p in range(zs):
                rowbuf[rows * p : rows * (p + 1), :] = zbuf[k, p].astype(F32)
            picked = jnp.dot(sel[...], rowbuf[...].astype(BF16), preferred_element_type=F32)
            ysend[k] = picked.astype(BF16).reshape(groups, slots, WIDTH)
            for p in y_peers:
                send(ysend.at[k, p], arrived.at[k, c, x, y], 2, y_sem.at[k], at(p, z, x, c))
            arrived[k, c, x, y] = ysend[k, y]

        @pl.when(t + 2 < chunks)
        def _():
            send_tokens(t + 2)

        @pl.when((t >= 1) & (t < chunks + 1))
        def _():
            k = t - 1
            wait(arrived.at[k, c, x, pl.ds(0, groups - 1)], y_sem.at[k])
            own = arrived.at[k, c, x]
            send(own, own, 3, b_sem.at[k], at(y, z, xf, c))
            send(own, own, 3, f_sem.at[k], at(y, z, xb, c))
            send(own, own, 4, core_sem.at[k], at(y, z, x, other))

        @pl.when((t >= 2) & (t < chunks + 2))
        def _():
            k = t - 2
            back = arrived.at[k, c, xb]
            wait(back, b_sem.at[k])
            send(back, back, 3, fwd_sem.at[k], at(y, z, xf, c))
            send(back, back, 4, core_sem.at[k], at(y, z, x, other))
            front = arrived.at[k, c, xf]
            wait(front, f_sem.at[k])
            send(front, front, 4, core_sem.at[k], at(y, z, x, other))

        @pl.when((t >= 3) & (t < chunks + 3))
        def _():
            k = t - 3
            block = arrived.at[k, c, far]
            wait(block, fwd_sem.at[k])
            send(block, block, 4, core_sem.at[k], at(y, z, x, other))

        @pl.when(t >= 4)
        def _():
            k = t - 4
            wait(arrived.at[k, other], core_sem.at[k])

            @pl.when(k == 0)
            def _():
                for copy in weights:
                    copy.wait()

            depth = pl.ds(pl.multiple_of(k * WIDTH, WIDTH), WIDTH)
            for half in range(CORES):
                flat = arrived[k, half].reshape(-1, WIDTH)
                acc_gate[half] += jnp.dot(flat, w_gate[depth, :], preferred_element_type=F32)
                acc_up[half] += jnp.dot(flat, w_up[depth, :], preferred_element_type=F32)

        return carry

    lax.fori_loop(0, chunks + 4, dispatch, 0)

    gate_val = acc_gate[...]
    hidden[...] = (gate_val / (F32(1.0) + jnp.exp(-gate_val)) * acc_up[...]).astype(BF16)
    wait(w_down, w_sem.at[2])

    def combine(t, carry):
        @pl.when(t < chunks)
        def _():
            k = t
            value = jnp.dot(hidden[other], w_down[k], preferred_element_type=F32)
            psend[k] = value.astype(BF16).reshape(psend.shape[1:])
            send(psend.at[k], pair.at[k], 5, pair_sem.at[k], at(y, z, x, other))

        @pl.when((t >= 1) & (t < chunks + 1))
        def _():
            k = t - 1
            value = jnp.dot(hidden[c], w_down[k], preferred_element_type=F32)
            part[...] = value.reshape(part.shape)
            wait(pair.at[k], pair_sem.at[k])
            send_far[k] = (part[far] + pair[k, far].astype(F32)).astype(BF16)
            send(send_far.at[k], got_far.at[k], 6, far_sem.at[k], at(y, z, xb, c))
            send_f[k] = (part[xf] + pair[k, xf].astype(F32)).astype(BF16)
            send(send_f.at[k], got_b.at[k], 9, rb_sem.at[k], at(y, z, xf, c))
            keep_b[k] = part[xb] + pair[k, xb].astype(F32)
            keep_own[k] = part[x] + pair[k, x].astype(F32)

        @pl.when((t >= 2) & (t < chunks + 2))
        def _():
            k = t - 2
            wait(got_far.at[k], far_sem.at[k])
            send_b[k] = (keep_b[k] + got_far[k].astype(F32)).astype(BF16)
            send(send_b.at[k], got_f.at[k], 10, rf_sem.at[k], at(y, z, xb, c))

        @pl.when((t >= 3) & (t < chunks + 3))
        def _():
            k = t - 3
            wait(got_b.at[k], rb_sem.at[k])
            wait(got_f.at[k], rf_sem.at[k])
            value = keep_own[k] + got_b[k].astype(F32) + got_f[k].astype(F32)
            vsend[k] = value.astype(BF16)
            for p in y_peers:
                send(vsend.at[k, p], vbuf.at[k, y], 7, v_sem.at[k], at(p, z, x, c))
            vbuf[k, y] = vsend[k, y]

        @pl.when((t >= 4) & (t < chunks + 4))
        def _():
            k = t - 4
            wait(vbuf.at[k, pl.ds(0, groups - 1)], v_sem.at[k])
            value = jnp.dot(mix[...], vbuf[k].reshape(-1, WIDTH), preferred_element_type=F32)
            for p in range(zs):
                msend[k, p] = value[rows * p : rows * (p + 1)].astype(BF16)
            for p in z_peers:
                send(msend.at[k, p], fbuf.at[k, z], 8, fin_sem.at[k], at(y, p, x, c))
            fbuf[k, z] = msend[k, z]

        @pl.when(t >= 5)
        def _():
            k = t - 5
            wait(fbuf.at[k, pl.ds(0, zs - 1)], fin_sem.at[k])
            value = fbuf[k, 0].astype(F32)
            for p in range(1, zs):
                value = value + fbuf[k, p].astype(F32)
            out_ref[:, pl.ds(pl.multiple_of(k * WIDTH, WIDTH), WIDTH)] = value.astype(BF16)

        return carry

    lax.fori_loop(0, chunks + 5, combine, 0)

    wait(meta.at[pl.ds(0, zs - 1)], send_sem.at[0])
    wait(zbuf.at[:, pl.ds(0, zs - 1)], send_sem.at[1])
    wait(ysend.at[:, pl.ds(0, groups - 1)], send_sem.at[2])
    wait(arrived.at[:, 0, pl.ds(0, 3)], send_sem.at[3])
    wait(arrived.at[:, 0], send_sem.at[4])
    wait(psend, send_sem.at[5])
    wait(send_far, send_sem.at[6])
    wait(send_f, send_sem.at[9])
    wait(send_b, send_sem.at[10])
    wait(vsend.at[:, pl.ds(0, groups - 1)], send_sem.at[7])
    wait(msend.at[:, pl.ds(0, zs - 1)], send_sem.at[8])


def on_device(tokens, expert_ids, gate_weights, w_gate, w_up, w_down):
    groups = lax.axis_size("group")
    members = lax.axis_size("expert")
    zs = EXP_GRP
    xs = members // (EXP_GRP * CORES)
    rows, width = tokens.shape
    block = w_gate.shape[2]
    chunks = width // WIDTH
    slots = zs * CAP
    shard = (groups, slots, WIDTH)
    vmem = pltpu.VMEM
    dma = pltpu.SemaphoreType.DMA
    in_vmem = pl.BlockSpec(memory_space=pltpu.VMEM)
    in_hbm = pl.BlockSpec(memory_space=pltpu.HBM)
    side = (CORES, xs * groups * slots, block)
    return pl.pallas_call(
        functools.partial(kernel, groups, zs, xs, rows, chunks),
        out_shape=jax.ShapeDtypeStruct((rows, width), BF16),
        in_specs=[in_vmem] * 3 + [in_hbm] * 3,
        out_specs=in_vmem,
        scratch_shapes=[
            vmem((width, block), BF16),
            vmem((width, block), BF16),
            vmem((chunks, block, WIDTH), BF16),
            vmem((chunks, zs, rows, WIDTH), BF16),
            vmem((zs, rows, 128), F32),
            vmem((zs * rows, WIDTH), F32),
            vmem((groups * slots, zs * rows), BF16),
            vmem((zs * rows, groups * slots), BF16),
            vmem((chunks,) + shard, BF16),
            vmem((chunks, CORES, xs) + shard, BF16),
            vmem(side, F32),
            vmem(side, F32),
            vmem(side, BF16),
            vmem((chunks, xs) + shard, BF16),
            vmem((chunks, xs) + shard, BF16),
            vmem((xs,) + shard, F32),
            vmem((chunks,) + shard, F32),
            vmem((chunks,) + shard, F32),
        ]
        + [vmem((chunks,) + shard, BF16)] * 8
        + [vmem((chunks, zs, rows, WIDTH), BF16)] * 2
        + [dma((3,)), dma]
        + [dma((chunks,))] * 12
        + [dma((11,))],
        compiler_params=pltpu.CompilerParams(
            collective_id=0, has_side_effects=True, vmem_limit_bytes=60 * 1024 * 1024
        ),
    )(tokens, expert_ids, gate_weights, w_gate, w_up, w_down)


def solution(mesh):
    in_specs = (
        P(("group", "expert"), None),
        P(("group", "expert"), None),
        P(("group", "expert"), None),
        P(("group", "expert"), None, None),
        P(("group", "expert"), None, None),
        P(("group", "expert"), None, None),
    )
    out_specs = P(("group", "expert"), None)
    return jax.shard_map(
        on_device, mesh=mesh, in_specs=in_specs, out_specs=out_specs, check_vma=False
    )
```

```python
import functools

import jax
import jax.numpy as jnp
from jax import lax
from jax.experimental import pallas as pl
from jax.experimental.pallas import tpu as pltpu
from jax.sharding import PartitionSpec as P

EXP_GRP = 8
CAP = 2
CORES = 2
WIDTH = 512
WIDE = 5
AHEAD = 9
EARLY = 9
LAGS = (0, 2, 5, 8, 9)
WIDE_LAGS = (0, 6, 9, 10)
BACK_LAGS = (0, 2, 5, 8, 10, 12)
WIDE_BACK_LAGS = (0, 2, 5, 8, 11)
MESH = pl.DeviceIdType.MESH
F32 = jnp.float32
BF16 = jnp.bfloat16


def routing_table(ids, gates, experts):
    rows, top = ids.shape
    lane = lax.broadcasted_iota(jnp.int32, (rows, 128), 1)
    named = jnp.zeros((rows, 128), F32)
    weight = jnp.zeros((rows, 128), F32)
    for k in range(top):
        chosen = ids[:, k : k + 1]
        named = jnp.where(lane == chosen, F32(1.0), named)
        weight = jnp.where(lane == chosen + experts, gates[:, k : k + 1], weight)
    earlier = jnp.zeros((1, 128), F32)
    out = []
    for row in range(rows):
        mine = named[row : row + 1]
        out.append(mine * (F32(1.0) + earlier) + weight[row : row + 1])
        earlier = earlier + mine
    return out


def kernel(
    groups, zs, xs, rows, chunks,
    tok_ref, ids_ref, gates_ref, gate_hbm, up_hbm, down_hbm, out_ref,
    w_gate, w_up, w_down, zbuf, zwide, meta, rowbuf, sel, mix, ysend, ywide, arrived,
    acc_gate, acc_up, hidden, psend, pair, part, keep_b, keep_own,
    send_far, send_f, send_b, got_far, got_f, got_b, vsend, vbuf, msend, fbuf,
    vwide, vgot, mwide, fgot, hsend, hgot,
    w_sem, meta_sem, metax_sem, z_sem, y_sem, b_sem, f_sem, fwd_sem,
    far_sem, rf_sem, rb_sem, v_sem, fin_sem,
    xw_sem, zw_sem, yw_sem, vw_sem, fw_sem, hw_sem,
    core_sem, pair_sem, send_sem,
):
    y = lax.axis_index("group")
    member = lax.axis_index("expert")
    z = member // (xs * CORES)
    x = (member // CORES) % xs
    c = member % CORES
    other = 1 - c
    step = 1 - 2 * c
    xf = (x + step + xs) % xs
    xb = (x - step + xs) % xs
    far = (x + 2) % xs
    experts = groups * EXP_GRP
    slots = zs * CAP
    wide = min(WIDE, chunks - 1)
    ring = chunks - wide

    def at(y_, z_, x_, c_):
        return (y_, (z_ * xs + x_) * CORES + c_)

    z_peers = [(z + d) % zs for d in range(1, zs)]
    y_peers = [(y + d) % groups for d in range(1, groups)]
    x_peers = [(x + d) % xs for d in range(1, xs)]

    def send(src, dst, which, recv, where):
        pltpu.make_async_remote_copy(
            src_ref=src, dst_ref=dst, send_sem=send_sem.at[which], recv_sem=recv,
            device_id=where, device_id_type=MESH,
        ).start()

    def wait(ref, sem):
        pltpu.make_async_copy(ref, ref, sem).wait()

    def columns(k):
        return pl.ds(pl.multiple_of(k * WIDTH, WIDTH), WIDTH)

    weights = [
        pltpu.make_async_copy(gate_hbm.at[0], w_gate, w_sem.at[0]),
        pltpu.make_async_copy(up_hbm.at[0], w_up, w_sem.at[1]),
    ]
    for copy in weights:
        copy.start()
    for k in range(chunks):
        pltpu.make_async_copy(
            down_hbm.at[0, :, pl.ds(k * WIDTH, WIDTH)], w_down.at[k], w_sem.at[2]
        ).start()

    barrier = pltpu.get_barrier_semaphore()
    partners = (
        [at(y, p, x, c) for p in z_peers]
        + [at(p, z, x, c) for p in y_peers]
        + [at(y, z, p, c) for p in x_peers]
        + [at(y, z, x, other)]
    )
    for p in partners:
        pl.semaphore_signal(barrier, inc=1, device_id=p, device_id_type=MESH)

    table = routing_table(ids_ref[...], gates_ref[...].astype(F32), experts)
    for row in range(rows):
        meta[x, z, row : row + 1, :] = table[row]
    for k in range(ring):
        zbuf[k, z] = tok_ref[:, k * WIDTH : (k + 1) * WIDTH]
    for k in range(ring, chunks):
        zwide[k - ring, z, x] = tok_ref[:, k * WIDTH : (k + 1) * WIDTH]
    acc_gate[...] = jnp.zeros_like(acc_gate)
    acc_up[...] = jnp.zeros_like(acc_up)
    pl.semaphore_wait(barrier, len(partners))

    for p in z_peers:
        send(meta.at[x, z], meta.at[x, z], 0, meta_sem, at(y, p, x, c))

    def send_z(k):
        for p in z_peers:
            send(zbuf.at[k, z], zbuf.at[k, z], 1, z_sem.at[k], at(y, p, x, c))

    for k in range(EARLY):
        send_z(k)

    def first_wide(k, carry):
        for p in x_peers:
            send(zwide.at[k, z, x], zwide.at[k, z, x], 11, xw_sem.at[k], at(y, z, p, c))
        return carry

    lax.fori_loop(0, wide, first_wide, 0)

    total = zs * rows
    n = groups * slots
    lane = lax.broadcasted_iota(jnp.int32, (total, 128), 1)
    row_id = lax.broadcasted_iota(jnp.int32, (total, n), 0)
    col_id = lax.broadcasted_iota(jnp.int32, (total, n), 1)
    same = (row_id // rows) == ((col_id % slots) // CAP)
    place = (col_id % CAP + 1).astype(F32)
    eye = (
        lax.broadcasted_iota(jnp.int32, (n, n), 0) == lax.broadcasted_iota(jnp.int32, (n, n), 1)
    ).astype(F32).astype(BF16)

    def choose(p):
        for q in range(zs):
            rowbuf[rows * q : rows * (q + 1), 0:128] = meta[p, q]
        line = rowbuf[:, 0:128]
        pick = jnp.zeros((total, n), F32)
        blend = jnp.zeros((total, n), F32)
        for q in range(groups):
            expert = q * EXP_GRP + z
            code = jnp.sum(jnp.where(lane == expert, line, F32(0.0)), axis=1, keepdims=True)
            weight = jnp.sum(
                jnp.where(lane == expert + experts, line, F32(0.0)), axis=1, keepdims=True
            )
            hit = same & (col_id // slots == q) & (code == place)
            pick = jnp.where(hit, F32(1.0), pick)
            blend = jnp.where(hit, weight, blend)
        mix[p] = blend.astype(BF16)
        sel[p] = lax.dot_general(
            eye, pick.astype(BF16), (((1,), (1,)), ((), ())), preferred_element_type=F32
        ).astype(BF16)

    wait(meta.at[x, pl.ds(0, zs - 1)], meta_sem)
    for p in x_peers:
        send(meta.at[x], meta.at[x], 12, metax_sem, at(y, z, p, c))
    for k in range(EARLY, AHEAD):
        send_z(k)
    choose(x)

    def multiply(k):
        wait(arrived.at[k, other], core_sem.at[k])
        for half in range(CORES):
            flat = arrived[k, half].reshape(-1, WIDTH)
            acc_gate[half] += jnp.dot(flat, w_gate[columns(k), :], preferred_element_type=F32)
            acc_up[half] += jnp.dot(flat, w_up[columns(k), :], preferred_element_type=F32)

    def run(t, lag, count, body):
        @pl.when((t >= lag) & (t < lag + count))
        def _():
            body(t - lag)

    def pick_rows(k):
        wait(zbuf.at[k, pl.ds(0, zs - 1)], z_sem.at[k])
        for p in range(zs):
            rowbuf[rows * p : rows * (p + 1), :] = zbuf[k, p].astype(F32)
        picked = jnp.dot(sel[x], rowbuf[...].astype(BF16), preferred_element_type=F32)
        ysend[k] = picked.astype(BF16).reshape(groups, slots, WIDTH)
        for p in y_peers:
            send(ysend.at[k, p], arrived.at[k, c, x, y], 2, y_sem.at[k], at(p, z, x, c))
        arrived[k, c, x, y] = ysend[k, y]

    def ring_start(k):
        wait(arrived.at[k, c, x, pl.ds(0, groups - 1)], y_sem.at[k])
        own = arrived.at[k, c, x]
        send(own, own, 3, b_sem.at[k], at(y, z, xf, c))
        send(own, own, 3, f_sem.at[k], at(y, z, xb, c))
        send(own, own, 4, core_sem.at[k], at(y, z, x, other))

    def ring_forward(k):
        back = arrived.at[k, c, xb]
        wait(back, b_sem.at[k])
        send(back, back, 3, fwd_sem.at[k], at(y, z, xf, c))
        send(back, back, 4, core_sem.at[k], at(y, z, x, other))
        front = arrived.at[k, c, xf]
        wait(front, f_sem.at[k])
        send(front, front, 4, core_sem.at[k], at(y, z, x, other))

    def ring_end(k):
        block = arrived.at[k, c, far]
        wait(block, fwd_sem.at[k])
        send(block, block, 4, core_sem.at[k], at(y, z, x, other))

    def wide_z(j):
        wait(zwide.at[j, z, pl.ds(0, xs - 1)], xw_sem.at[j])
        for p in z_peers:
            send(zwide.at[j, z], zwide.at[j, z], 13, zw_sem.at[j], at(y, p, x, c))

    def wide_pick(j):
        @pl.when(j == 0)
        def _():
            wait(meta.at[pl.ds(0, xs - 1)], metax_sem)
            for p in x_peers:
                choose(p)

        wait(zwide.at[j, pl.ds(0, zs - 1)], zw_sem.at[j])
        k = ring + j
        for p in range(xs):
            for q in range(zs):
                rowbuf[rows * q : rows * (q + 1), :] = zwide[j, q, p].astype(F32)
            picked = jnp.dot(sel[p], rowbuf[...].astype(BF16), preferred_element_type=F32)
            picked = picked.astype(BF16).reshape(groups, slots, WIDTH)
            for q in range(groups):
                ywide[j, q, p] = picked[q]
        for p in y_peers:
            send(ywide.at[j, p], arrived.at[k, c, :, y], 14, yw_sem.at[j], at(p, z, x, c))
        for p in range(xs):
            arrived[k, c, p, y] = ywide[j, y, p]

    def wide_share(j):
        k = ring + j
        wait(arrived.at[k, c, pl.ds(0, groups - 1)], yw_sem.at[j])
        block = arrived.at[k, c]
        send(block, block, 4, core_sem.at[k], at(y, z, x, other))

    def loaded(j):
        for copy in weights:
            copy.wait()

    def dispatch(t, carry):
        run(t, LAGS[0], ring, pick_rows)
        run(t, LAGS[0], ring - AHEAD, lambda k: send_z(k + AHEAD))
        run(t, LAGS[1], ring, ring_start)
        run(t, WIDE_LAGS[0], wide, wide_z)
        run(t, LAGS[2], ring, ring_forward)
        run(t, WIDE_LAGS[1], wide, wide_pick)
        run(t, LAGS[3], ring, ring_end)
        run(t, WIDE_LAGS[2], wide, wide_share)
        run(t, min(LAGS[-1], WIDE_LAGS[-1]), 1, loaded)
        run(t, LAGS[4], ring, multiply)
        run(t, WIDE_LAGS[3], wide, lambda j: multiply(ring + j))
        return carry

    lax.fori_loop(0, max(ring + LAGS[-1], wide + WIDE_LAGS[-1]), dispatch, 0)

    gate_val = acc_gate[...]
    hidden[...] = (gate_val / (F32(1.0) + jnp.exp(-gate_val)) * acc_up[...]).astype(BF16)
    wait(w_down, w_sem.at[2])

    def partial_sum(k):
        value = jnp.dot(hidden[other], w_down[k], preferred_element_type=F32)
        psend[k] = value.astype(BF16).reshape(psend.shape[1:])
        send(psend.at[k], pair.at[k], 5, pair_sem.at[k], at(y, z, x, other))

    def reduce_start(k):
        value = jnp.dot(hidden[c], w_down[k], preferred_element_type=F32)
        part[...] = value.reshape(part.shape)
        wait(pair.at[k], pair_sem.at[k])
        send_far[k] = (part[far] + pair[k, far].astype(F32)).astype(BF16)
        send(send_far.at[k], got_far.at[k], 6, far_sem.at[k], at(y, z, xb, c))
        send_f[k] = (part[xf] + pair[k, xf].astype(F32)).astype(BF16)
        send(send_f.at[k], got_b.at[k], 9, rb_sem.at[k], at(y, z, xf, c))
        keep_b[k] = part[xb] + pair[k, xb].astype(F32)
        keep_own[k] = part[x] + pair[k, x].astype(F32)

    def reduce_forward(k):
        wait(got_far.at[k], far_sem.at[k])
        send_b[k] = (keep_b[k] + got_far[k].astype(F32)).astype(BF16)
        send(send_b.at[k], got_f.at[k], 10, rf_sem.at[k], at(y, z, xb, c))

    def reduce_end(k):
        wait(got_b.at[k], rb_sem.at[k])
        wait(got_f.at[k], rf_sem.at[k])
        value = keep_own[k] + got_b[k].astype(F32) + got_f[k].astype(F32)
        vsend[k] = value.astype(BF16)
        for p in y_peers:
            send(vsend.at[k, p], vbuf.at[k, y], 7, v_sem.at[k], at(p, z, x, c))
        vbuf[k, y] = vsend[k, y]

    def blend_rows(k):
        wait(vbuf.at[k, pl.ds(0, groups - 1)], v_sem.at[k])
        value = jnp.dot(mix[x], vbuf[k].reshape(-1, WIDTH), preferred_element_type=F32)
        for p in range(zs):
            msend[k, p] = value[rows * p : rows * (p + 1)].astype(BF16)
        for p in z_peers:
            send(msend.at[k, p], fbuf.at[k, z], 8, fin_sem.at[k], at(y, p, x, c))
        fbuf[k, z] = msend[k, z]

    def finish(k):
        wait(fbuf.at[k, pl.ds(0, zs - 1)], fin_sem.at[k])
        value = fbuf[k, 0].astype(F32)
        for p in range(1, zs):
            value = value + fbuf[k, p].astype(F32)
        out_ref[:, columns(k)] = value.astype(BF16)

    def wide_back(j):
        k = ring + j
        value = jnp.dot(hidden[c], w_down[k], preferred_element_type=F32)
        part[...] = value.reshape(part.shape)
        wait(pair.at[k], pair_sem.at[k])
        for p in range(xs):
            summed = (part[p] + pair[k, p].astype(F32)).astype(BF16)
            for q in range(groups):
                vwide[j, q, p] = summed[q]
        for p in y_peers:
            send(vwide.at[j, p], vgot.at[j, y], 15, vw_sem.at[j], at(p, z, x, c))
        vgot[j, y] = vwide[j, y]

    def wide_blend(j):
        wait(vgot.at[j, pl.ds(0, groups - 1)], vw_sem.at[j])
        for p in range(xs):
            value = jnp.dot(mix[p], vgot[j, :, p].reshape(-1, WIDTH), preferred_element_type=F32)
            for q in range(zs):
                mwide[j, q, p] = value[rows * q : rows * (q + 1)].astype(BF16)
        for p in z_peers:
            send(mwide.at[j, p], fgot.at[j, z], 16, fw_sem.at[j], at(y, p, x, c))
        fgot[j, z] = mwide[j, z]

    def wide_sum(j):
        wait(fgot.at[j, pl.ds(0, zs - 1)], fw_sem.at[j])
        value = fgot[j, 0].astype(F32)
        for p in range(1, zs):
            value = value + fgot[j, p].astype(F32)
        hsend[j] = value.astype(BF16)
        for p in x_peers:
            send(hsend.at[j, p], hgot.at[j, x], 17, hw_sem.at[j], at(y, z, p, c))
        hgot[j, x] = hsend[j, x]

    def wide_finish(j):
        wait(hgot.at[j, pl.ds(0, xs - 1)], hw_sem.at[j])
        value = hgot[j, 0].astype(F32)
        for p in range(1, xs):
            value = value + hgot[j, p].astype(F32)
        out_ref[:, columns(ring + j)] = value.astype(BF16)

    def combine(t, carry):
        run(t, BACK_LAGS[0], ring, partial_sum)
        run(t, WIDE_BACK_LAGS[0], wide, lambda j: partial_sum(ring + j))
        run(t, BACK_LAGS[1], ring, reduce_start)
        run(t, WIDE_BACK_LAGS[1], wide, wide_back)
        run(t, BACK_LAGS[2], ring, reduce_forward)
        run(t, WIDE_BACK_LAGS[2], wide, wide_blend)
        run(t, BACK_LAGS[3], ring, reduce_end)
        run(t, WIDE_BACK_LAGS[3], wide, wide_sum)
        run(t, BACK_LAGS[4], ring, blend_rows)
        run(t, WIDE_BACK_LAGS[4], wide, wide_finish)
        run(t, BACK_LAGS[5], ring, finish)
        return carry

    lax.fori_loop(0, max(ring + BACK_LAGS[-1], wide + WIDE_BACK_LAGS[-1]), combine, 0)

    wait(meta.at[x, pl.ds(0, zs - 1)], send_sem.at[0])
    wait(zbuf.at[:, pl.ds(0, zs - 1)], send_sem.at[1])
    wait(ysend.at[:, pl.ds(0, groups - 1)], send_sem.at[2])
    wait(arrived.at[pl.ds(0, ring), 0, pl.ds(0, 3)], send_sem.at[3])
    wait(arrived.at[:, 0], send_sem.at[4])
    wait(psend, send_sem.at[5])
    wait(send_far, send_sem.at[6])
    wait(vsend.at[:, pl.ds(0, groups - 1)], send_sem.at[7])
    wait(msend.at[:, pl.ds(0, zs - 1)], send_sem.at[8])
    wait(send_f, send_sem.at[9])
    wait(send_b, send_sem.at[10])
    wait(zwide.at[:, 0, pl.ds(0, xs - 1)], send_sem.at[11])
    wait(meta.at[pl.ds(0, xs - 1)], send_sem.at[12])
    wait(zwide.at[:, pl.ds(0, zs - 1)], send_sem.at[13])
    wait(ywide.at[:, pl.ds(0, groups - 1)], send_sem.at[14])
    wait(vwide.at[:, pl.ds(0, groups - 1)], send_sem.at[15])
    wait(mwide.at[:, pl.ds(0, zs - 1)], send_sem.at[16])
    wait(hsend.at[:, pl.ds(0, xs - 1)], send_sem.at[17])


def on_device(tokens, expert_ids, gate_weights, w_gate, w_up, w_down):
    groups = lax.axis_size("group")
    members = lax.axis_size("expert")
    zs = EXP_GRP
    xs = members // (EXP_GRP * CORES)
    rows, width = tokens.shape
    block = w_gate.shape[2]
    chunks = width // WIDTH
    wide = min(WIDE, chunks - 1)
    ring = chunks - wide
    slots = zs * CAP
    shard = (groups, slots, WIDTH)
    vmem = pltpu.VMEM
    dma = pltpu.SemaphoreType.DMA
    in_vmem = pl.BlockSpec(memory_space=pltpu.VMEM)
    in_hbm = pl.BlockSpec(memory_space=pltpu.HBM)
    side = (CORES, xs * groups * slots, block)
    return pl.pallas_call(
        functools.partial(kernel, groups, zs, xs, rows, chunks),
        out_shape=jax.ShapeDtypeStruct((rows, width), BF16),
        in_specs=[in_vmem] * 3 + [in_hbm] * 3,
        out_specs=in_vmem,
        scratch_shapes=[
            vmem((width, block), BF16),
            vmem((width, block), BF16),
            vmem((chunks, block, WIDTH), BF16),
            vmem((ring, zs, rows, WIDTH), BF16),
            vmem((wide, zs, xs, rows, WIDTH), BF16),
            vmem((xs, zs, rows, 128), F32),
            vmem((zs * rows, WIDTH), F32),
            vmem((xs, groups * slots, zs * rows), BF16),
            vmem((xs, zs * rows, groups * slots), BF16),
            vmem((ring,) + shard, BF16),
            vmem((wide, groups, xs, slots, WIDTH), BF16),
            vmem((chunks, CORES, xs) + shard, BF16),
            vmem(side, F32),
            vmem(side, F32),
            vmem(side, BF16),
            vmem((chunks, xs) + shard, BF16),
            vmem((chunks, xs) + shard, BF16),
            vmem((xs,) + shard, F32),
            vmem((ring,) + shard, F32),
            vmem((ring,) + shard, F32),
        ]
        + [vmem((ring,) + shard, BF16)] * 8
        + [vmem((ring, zs, rows, WIDTH), BF16)] * 2
        + [vmem((wide, groups, xs, slots, WIDTH), BF16)] * 2
        + [vmem((wide, zs, xs, rows, WIDTH), BF16)] * 2
        + [vmem((wide, xs, rows, WIDTH), BF16)] * 2
        + [dma((3,)), dma, dma]
        + [dma((ring,))] * 10
        + [dma((wide,))] * 6
        + [dma((chunks,))] * 2
        + [dma((18,))],
        compiler_params=pltpu.CompilerParams(
            collective_id=0, has_side_effects=True, vmem_limit_bytes=60 * 1024 * 1024
        ),
    )(tokens, expert_ids, gate_weights, w_gate, w_up, w_down)


def solution(mesh):
    in_specs = (
        P(("group", "expert"), None),
        P(("group", "expert"), None),
        P(("group", "expert"), None),
        P(("group", "expert"), None, None),
        P(("group", "expert"), None, None),
        P(("group", "expert"), None, None),
    )
    out_specs = P(("group", "expert"), None)
    return jax.shard_map(
        on_device, mesh=mesh, in_specs=in_specs, out_specs=out_specs, check_vma=False
    )
```

```python
import functools

import jax
import jax.numpy as jnp
from jax import lax
from jax.experimental import pallas as pl
from jax.experimental.pallas import tpu as pltpu
from jax.sharding import PartitionSpec as P

EXP_GRP = 8
CAP = 2
CORES = 2
WIDTH = 512
WIDE = 5
DIRECT = 1
STRIDE = 2
AHEAD = 9
EARLY = 9
LAGS = (0, 2, 5, 8, 9)
WIDE_LAGS = (0, 5, 8, 9)
BACK_LAGS = (0, 2, 5, 8, 10, 12)
WIDE_BACK_LAGS = (0, 1, 5, 9, 12)
MESH = pl.DeviceIdType.MESH
F32 = jnp.float32
BF16 = jnp.bfloat16


def routing_table(ids, gates, experts):
    rows, top = ids.shape
    lane = lax.broadcasted_iota(jnp.int32, (rows, 128), 1)
    named = jnp.zeros((rows, 128), F32)
    weight = jnp.zeros((rows, 128), F32)
    for k in range(top):
        chosen = ids[:, k : k + 1]
        named = jnp.where(lane == chosen, F32(1.0), named)
        weight = jnp.where(lane == chosen + experts, gates[:, k : k + 1], weight)
    earlier = jnp.zeros((1, 128), F32)
    out = []
    for row in range(rows):
        mine = named[row : row + 1]
        out.append(mine * (F32(1.0) + earlier) + weight[row : row + 1])
        earlier = earlier + mine
    return out


def kernel(
    groups, zs, xs, rows, chunks,
    tok_ref, ids_ref, gates_ref, gate_hbm, up_hbm, down_hbm, out_ref,
    w_gate, w_up, w_down, zbuf, zwide, meta, rowbuf, sel, mix, ysend, ywide, arrived,
    acc_gate, acc_up, hidden, psend, pair, part, keep_b, keep_own,
    send_far, send_f, send_b, got_far, got_f, got_b, vsend, vbuf, msend, fbuf,
    vwide, vgot, mwide, fgot, hsend, hgot,
    w_sem, meta_sem, metax_sem, z_sem, y_sem, b_sem, f_sem, fwd_sem,
    far_sem, rf_sem, rb_sem, v_sem, fin_sem,
    xw_sem, zw_sem, yw_sem, vw_sem, fw_sem, hw_sem,
    core_sem, pair_sem, send_sem,
):
    y = lax.axis_index("group")
    member = lax.axis_index("expert")
    z = member // (xs * CORES)
    x = (member // CORES) % xs
    c = member % CORES
    other = 1 - c
    step = 1 - 2 * c
    xf = (x + step + xs) % xs
    xb = (x - step + xs) % xs
    far = (x + 2) % xs
    experts = groups * EXP_GRP
    slots = zs * CAP
    wide = min(WIDE, chunks - 1)
    ring = chunks - wide
    relayed = ring - DIRECT

    def at(y_, z_, x_, c_):
        return (y_, (z_ * xs + x_) * CORES + c_)

    z_peers = [(z + d) % zs for d in range(1, zs)]
    y_peers = [(y + d) % groups for d in range(1, groups)]
    x_peers = [(x + d) % xs for d in range(1, xs)]

    def send(src, dst, which, recv, where):
        pltpu.make_async_remote_copy(
            src_ref=src, dst_ref=dst, send_sem=send_sem.at[which], recv_sem=recv,
            device_id=where, device_id_type=MESH,
        ).start()

    def wait(ref, sem):
        pltpu.make_async_copy(ref, ref, sem).wait()

    def columns(k):
        return pl.ds(pl.multiple_of(k * WIDTH, WIDTH), WIDTH)

    weights = [
        pltpu.make_async_copy(gate_hbm.at[0], w_gate, w_sem.at[0]),
        pltpu.make_async_copy(up_hbm.at[0], w_up, w_sem.at[1]),
    ]
    for copy in weights:
        copy.start()
    for k in range(chunks):
        pltpu.make_async_copy(
            down_hbm.at[0, :, pl.ds(k * WIDTH, WIDTH)], w_down.at[k], w_sem.at[2]
        ).start()

    barrier = pltpu.get_barrier_semaphore()
    partners = (
        [at(y, p, x, c) for p in z_peers]
        + [at(p, z, x, c) for p in y_peers]
        + [at(y, z, p, c) for p in x_peers]
        + [at(y, z, x, other)]
    )
    for p in partners:
        pl.semaphore_signal(barrier, inc=1, device_id=p, device_id_type=MESH)

    table = routing_table(ids_ref[...], gates_ref[...].astype(F32), experts)
    for row in range(rows):
        meta[x, z, row : row + 1, :] = table[row]
    for k in range(ring):
        zbuf[k, z] = tok_ref[:, k * WIDTH : (k + 1) * WIDTH]
    for k in range(ring, chunks):
        zwide[k - ring, z, x] = tok_ref[:, k * WIDTH : (k + 1) * WIDTH]
    acc_gate[...] = jnp.zeros_like(acc_gate)
    acc_up[...] = jnp.zeros_like(acc_up)
    pl.semaphore_wait(barrier, len(partners))

    for p in z_peers:
        send(meta.at[x, z], meta.at[x, z], 0, meta_sem, at(y, p, x, c))

    def send_z(k):
        for p in z_peers:
            send(zbuf.at[k, z], zbuf.at[k, z], 1, z_sem.at[k], at(y, p, x, c))

    for k in range(EARLY):
        send_z(k)

    def first_wide(k, carry):
        for p in x_peers:
            send(zwide.at[k, z, x], zwide.at[k, z, x], 11, xw_sem.at[k], at(y, z, p, c))
        return carry

    lax.fori_loop(0, wide, first_wide, 0)

    total = zs * rows
    n = groups * slots
    lane = lax.broadcasted_iota(jnp.int32, (total, 128), 1)
    row_id = lax.broadcasted_iota(jnp.int32, (total, n), 0)
    col_id = lax.broadcasted_iota(jnp.int32, (total, n), 1)
    same = (row_id // rows) == ((col_id % slots) // CAP)
    place = (col_id % CAP + 1).astype(F32)
    eye = (
        lax.broadcasted_iota(jnp.int32, (n, n), 0) == lax.broadcasted_iota(jnp.int32, (n, n), 1)
    ).astype(F32).astype(BF16)

    def choose(p):
        for q in range(zs):
            rowbuf[rows * q : rows * (q + 1), 0:128] = meta[p, q]
        line = rowbuf[:, 0:128]
        pick = jnp.zeros((total, n), F32)
        blend = jnp.zeros((total, n), F32)
        for q in range(groups):
            expert = q * EXP_GRP + z
            code = jnp.sum(jnp.where(lane == expert, line, F32(0.0)), axis=1, keepdims=True)
            weight = jnp.sum(
                jnp.where(lane == expert + experts, line, F32(0.0)), axis=1, keepdims=True
            )
            hit = same & (col_id // slots == q) & (code == place)
            pick = jnp.where(hit, F32(1.0), pick)
            blend = jnp.where(hit, weight, blend)
        mix[p] = blend.astype(BF16)
        sel[p] = lax.dot_general(
            eye, pick.astype(BF16), (((1,), (1,)), ((), ())), preferred_element_type=F32
        ).astype(BF16)

    wait(meta.at[x, pl.ds(0, zs - 1)], meta_sem)
    for p in x_peers:
        send(meta.at[x], meta.at[x], 12, metax_sem, at(y, z, p, c))
    for k in range(EARLY, AHEAD):
        send_z(k)
    choose(x)

    def multiply(k):
        wait(arrived.at[k, other], core_sem.at[k])
        for half in range(CORES):
            flat = arrived[k, half].reshape(-1, WIDTH)
            acc_gate[half] += jnp.dot(flat, w_gate[columns(k), :], preferred_element_type=F32)
            acc_up[half] += jnp.dot(flat, w_up[columns(k), :], preferred_element_type=F32)

    def run(t, lag, count, body):
        @pl.when((t >= lag) & (t < lag + count))
        def _():
            body(t - lag)

    def run_wide(t, lag, body):
        @pl.when((t >= lag) & (t < lag + wide * STRIDE) & ((t - lag) % STRIDE == 0))
        def _():
            body((t - lag) // STRIDE)

    def pick_rows(k):
        wait(zbuf.at[k, pl.ds(0, zs - 1)], z_sem.at[k])
        for p in range(zs):
            rowbuf[rows * p : rows * (p + 1), :] = zbuf[k, p].astype(F32)
        picked = jnp.dot(sel[x], rowbuf[...].astype(BF16), preferred_element_type=F32)
        ysend[k] = picked.astype(BF16).reshape(groups, slots, WIDTH)
        for p in y_peers:
            send(ysend.at[k, p], arrived.at[k, c, x, y], 2, y_sem.at[k], at(p, z, x, c))
        arrived[k, c, x, y] = ysend[k, y]

    def ring_start(k):
        wait(arrived.at[k, c, x, pl.ds(0, groups - 1)], y_sem.at[k])
        own = arrived.at[k, c, x]
        send(own, own, 3, b_sem.at[k], at(y, z, xf, c))
        send(own, own, 3, f_sem.at[k], at(y, z, xb, c))
        send(own, own, 4, core_sem.at[k], at(y, z, x, other))

        @pl.when(k >= relayed)
        def _():
            send(own, own, 3, fwd_sem.at[k], at(y, z, far, c))

    def ring_forward(k):
        back = arrived.at[k, c, xb]
        wait(back, b_sem.at[k])

        @pl.when(k < relayed)
        def _():
            send(back, back, 3, fwd_sem.at[k], at(y, z, xf, c))

        send(back, back, 4, core_sem.at[k], at(y, z, x, other))
        front = arrived.at[k, c, xf]
        wait(front, f_sem.at[k])
        send(front, front, 4, core_sem.at[k], at(y, z, x, other))

    def ring_end(k):
        block = arrived.at[k, c, far]
        wait(block, fwd_sem.at[k])
        send(block, block, 4, core_sem.at[k], at(y, z, x, other))

    def wide_z(j):
        wait(zwide.at[j, z, pl.ds(0, xs - 1)], xw_sem.at[j])
        for p in z_peers:
            send(zwide.at[j, z], zwide.at[j, z], 13, zw_sem.at[j], at(y, p, x, c))

    def wide_pick(j):
        @pl.when(j == 0)
        def _():
            wait(meta.at[pl.ds(0, xs - 1)], metax_sem)
            for p in x_peers:
                choose(p)

        wait(zwide.at[j, pl.ds(0, zs - 1)], zw_sem.at[j])
        k = ring + j
        for p in range(xs):
            for q in range(zs):
                rowbuf[rows * q : rows * (q + 1), :] = zwide[j, q, p].astype(F32)
            picked = jnp.dot(sel[p], rowbuf[...].astype(BF16), preferred_element_type=F32)
            picked = picked.astype(BF16).reshape(groups, slots, WIDTH)
            for q in range(groups):
                ywide[j, q, p] = picked[q]
        for p in y_peers:
            send(ywide.at[j, p], arrived.at[k, c, :, y], 14, yw_sem.at[j], at(p, z, x, c))
        for p in range(xs):
            arrived[k, c, p, y] = ywide[j, y, p]

    def wide_share(j):
        k = ring + j
        wait(arrived.at[k, c, pl.ds(0, groups - 1)], yw_sem.at[j])
        block = arrived.at[k, c]
        send(block, block, 4, core_sem.at[k], at(y, z, x, other))

    def loaded(j):
        for copy in weights:
            copy.wait()

    def dispatch(t, carry):
        run(t, LAGS[0], ring, pick_rows)
        run(t, LAGS[0], ring - AHEAD, lambda k: send_z(k + AHEAD))
        run(t, LAGS[1], ring, ring_start)
        run_wide(t, WIDE_LAGS[0], wide_z)
        run(t, LAGS[2], ring, ring_forward)
        run_wide(t, WIDE_LAGS[1], wide_pick)
        run(t, LAGS[3], ring, ring_end)
        run_wide(t, WIDE_LAGS[2], wide_share)
        run(t, min(LAGS[-1], WIDE_LAGS[-1]), 1, loaded)
        run(t, LAGS[4], ring, multiply)
        run_wide(t, WIDE_LAGS[3], lambda j: multiply(ring + j))
        return carry

    lax.fori_loop(0, max(ring + LAGS[-1], wide * STRIDE + WIDE_LAGS[-1]), dispatch, 0)

    gate_val = acc_gate[...]
    hidden[...] = (gate_val / (F32(1.0) + jnp.exp(-gate_val)) * acc_up[...]).astype(BF16)
    wait(w_down, w_sem.at[2])

    def partial_sum(k):
        value = jnp.dot(hidden[other], w_down[k], preferred_element_type=F32)
        psend[k] = value.astype(BF16).reshape(psend.shape[1:])
        send(psend.at[k], pair.at[k], 5, pair_sem.at[k], at(y, z, x, other))

    def reduce_start(k):
        value = jnp.dot(hidden[c], w_down[k], preferred_element_type=F32)
        part[...] = value.reshape(part.shape)
        wait(pair.at[k], pair_sem.at[k])
        send_far[k] = (part[far] + pair[k, far].astype(F32)).astype(BF16)

        @pl.when(k < relayed)
        def _():
            send(send_far.at[k], got_far.at[k], 6, far_sem.at[k], at(y, z, xb, c))

        @pl.when(k >= relayed)
        def _():
            send(send_far.at[k], got_far.at[k], 6, far_sem.at[k], at(y, z, far, c))
            send_b[k] = (part[xb] + pair[k, xb].astype(F32)).astype(BF16)
            send(send_b.at[k], got_f.at[k], 10, rf_sem.at[k], at(y, z, xb, c))

        send_f[k] = (part[xf] + pair[k, xf].astype(F32)).astype(BF16)
        send(send_f.at[k], got_b.at[k], 9, rb_sem.at[k], at(y, z, xf, c))
        keep_b[k] = part[xb] + pair[k, xb].astype(F32)
        keep_own[k] = part[x] + pair[k, x].astype(F32)

    def reduce_forward(k):
        wait(got_far.at[k], far_sem.at[k])
        send_b[k] = (keep_b[k] + got_far[k].astype(F32)).astype(BF16)
        send(send_b.at[k], got_f.at[k], 10, rf_sem.at[k], at(y, z, xb, c))

    def reduce_end(k):
        @pl.when(k >= relayed)
        def _():
            wait(got_far.at[k], far_sem.at[k])
            keep_own[k] = keep_own[k] + got_far[k].astype(F32)

        wait(got_b.at[k], rb_sem.at[k])
        wait(got_f.at[k], rf_sem.at[k])
        value = keep_own[k] + got_b[k].astype(F32) + got_f[k].astype(F32)
        vsend[k] = value.astype(BF16)
        for p in y_peers:
            send(vsend.at[k, p], vbuf.at[k, y], 7, v_sem.at[k], at(p, z, x, c))
        vbuf[k, y] = vsend[k, y]

    def blend_rows(k):
        wait(vbuf.at[k, pl.ds(0, groups - 1)], v_sem.at[k])
        value = jnp.dot(mix[x], vbuf[k].reshape(-1, WIDTH), preferred_element_type=F32)
        for p in range(zs):
            msend[k, p] = value[rows * p : rows * (p + 1)].astype(BF16)
        for p in z_peers:
            send(msend.at[k, p], fbuf.at[k, z], 8, fin_sem.at[k], at(y, p, x, c))
        fbuf[k, z] = msend[k, z]

    def finish(k):
        wait(fbuf.at[k, pl.ds(0, zs - 1)], fin_sem.at[k])
        value = fbuf[k, 0].astype(F32)
        for p in range(1, zs):
            value = value + fbuf[k, p].astype(F32)
        out_ref[:, columns(k)] = value.astype(BF16)

    def wide_back(j):
        k = ring + j
        value = jnp.dot(hidden[c], w_down[k], preferred_element_type=F32)
        part[...] = value.reshape(part.shape)
        wait(pair.at[k], pair_sem.at[k])
        for p in range(xs):
            summed = (part[p] + pair[k, p].astype(F32)).astype(BF16)
            for q in range(groups):
                vwide[j, q, p] = summed[q]
        for p in y_peers:
            send(vwide.at[j, p], vgot.at[j, y], 15, vw_sem.at[j], at(p, z, x, c))
        vgot[j, y] = vwide[j, y]

    def wide_blend(j):
        wait(vgot.at[j, pl.ds(0, groups - 1)], vw_sem.at[j])
        for p in range(xs):
            value = jnp.dot(mix[p], vgot[j, :, p].reshape(-1, WIDTH), preferred_element_type=F32)
            for q in range(zs):
                mwide[j, q, p] = value[rows * q : rows * (q + 1)].astype(BF16)
        for p in z_peers:
            send(mwide.at[j, p], fgot.at[j, z], 16, fw_sem.at[j], at(y, p, x, c))
        fgot[j, z] = mwide[j, z]

    def wide_sum(j):
        wait(fgot.at[j, pl.ds(0, zs - 1)], fw_sem.at[j])
        value = fgot[j, 0].astype(F32)
        for p in range(1, zs):
            value = value + fgot[j, p].astype(F32)
        hsend[j] = value.astype(BF16)
        for p in x_peers:
            send(hsend.at[j, p], hgot.at[j, x], 17, hw_sem.at[j], at(y, z, p, c))
        hgot[j, x] = hsend[j, x]

    def wide_finish(j):
        wait(hgot.at[j, pl.ds(0, xs - 1)], hw_sem.at[j])
        value = hgot[j, 0].astype(F32)
        for p in range(1, xs):
            value = value + hgot[j, p].astype(F32)
        out_ref[:, columns(ring + j)] = value.astype(BF16)

    def combine(t, carry):
        run(t, BACK_LAGS[0], ring, partial_sum)
        run_wide(t, WIDE_BACK_LAGS[0], lambda j: partial_sum(ring + j))
        run(t, BACK_LAGS[1], ring, reduce_start)
        run_wide(t, WIDE_BACK_LAGS[1], wide_back)
        run(t, BACK_LAGS[2], relayed, reduce_forward)
        run_wide(t, WIDE_BACK_LAGS[2], wide_blend)
        run(t, BACK_LAGS[3], ring, reduce_end)
        run_wide(t, WIDE_BACK_LAGS[3], wide_sum)
        run(t, BACK_LAGS[4], ring, blend_rows)
        run_wide(t, WIDE_BACK_LAGS[4], wide_finish)
        run(t, BACK_LAGS[5], ring, finish)
        return carry

    lax.fori_loop(0, max(ring + BACK_LAGS[-1], wide * STRIDE + WIDE_BACK_LAGS[-1]), combine, 0)

    wait(meta.at[x, pl.ds(0, zs - 1)], send_sem.at[0])
    wait(zbuf.at[:, pl.ds(0, zs - 1)], send_sem.at[1])
    wait(ysend.at[:, pl.ds(0, groups - 1)], send_sem.at[2])
    wait(arrived.at[pl.ds(0, ring), 0, pl.ds(0, 3)], send_sem.at[3])
    wait(arrived.at[:, 0], send_sem.at[4])
    wait(psend, send_sem.at[5])
    wait(send_far, send_sem.at[6])
    wait(vsend.at[:, pl.ds(0, groups - 1)], send_sem.at[7])
    wait(msend.at[:, pl.ds(0, zs - 1)], send_sem.at[8])
    wait(send_f, send_sem.at[9])
    wait(send_b, send_sem.at[10])
    wait(zwide.at[:, 0, pl.ds(0, xs - 1)], send_sem.at[11])
    wait(meta.at[pl.ds(0, xs - 1)], send_sem.at[12])
    wait(zwide.at[:, pl.ds(0, zs - 1)], send_sem.at[13])
    wait(ywide.at[:, pl.ds(0, groups - 1)], send_sem.at[14])
    wait(vwide.at[:, pl.ds(0, groups - 1)], send_sem.at[15])
    wait(mwide.at[:, pl.ds(0, zs - 1)], send_sem.at[16])
    wait(hsend.at[:, pl.ds(0, xs - 1)], send_sem.at[17])


def on_device(tokens, expert_ids, gate_weights, w_gate, w_up, w_down):
    groups = lax.axis_size("group")
    members = lax.axis_size("expert")
    zs = EXP_GRP
    xs = members // (EXP_GRP * CORES)
    rows, width = tokens.shape
    block = w_gate.shape[2]
    chunks = width // WIDTH
    wide = min(WIDE, chunks - 1)
    ring = chunks - wide
    slots = zs * CAP
    shard = (groups, slots, WIDTH)
    vmem = pltpu.VMEM
    dma = pltpu.SemaphoreType.DMA
    in_vmem = pl.BlockSpec(memory_space=pltpu.VMEM)
    in_hbm = pl.BlockSpec(memory_space=pltpu.HBM)
    side = (CORES, xs * groups * slots, block)
    return pl.pallas_call(
        functools.partial(kernel, groups, zs, xs, rows, chunks),
        out_shape=jax.ShapeDtypeStruct((rows, width), BF16),
        in_specs=[in_vmem] * 3 + [in_hbm] * 3,
        out_specs=in_vmem,
        scratch_shapes=[
            vmem((width, block), BF16),
            vmem((width, block), BF16),
            vmem((chunks, block, WIDTH), BF16),
            vmem((ring, zs, rows, WIDTH), BF16),
            vmem((wide, zs, xs, rows, WIDTH), BF16),
            vmem((xs, zs, rows, 128), F32),
            vmem((zs * rows, WIDTH), F32),
            vmem((xs, groups * slots, zs * rows), BF16),
            vmem((xs, zs * rows, groups * slots), BF16),
            vmem((ring,) + shard, BF16),
            vmem((wide, groups, xs, slots, WIDTH), BF16),
            vmem((chunks, CORES, xs) + shard, BF16),
            vmem(side, F32),
            vmem(side, F32),
            vmem(side, BF16),
            vmem((chunks, xs) + shard, BF16),
            vmem((chunks, xs) + shard, BF16),
            vmem((xs,) + shard, F32),
            vmem((ring,) + shard, F32),
            vmem((ring,) + shard, F32),
        ]
        + [vmem((ring,) + shard, BF16)] * 8
        + [vmem((ring, zs, rows, WIDTH), BF16)] * 2
        + [vmem((wide, groups, xs, slots, WIDTH), BF16)] * 2
        + [vmem((wide, zs, xs, rows, WIDTH), BF16)] * 2
        + [vmem((wide, xs, rows, WIDTH), BF16)] * 2
        + [dma((3,)), dma, dma]
        + [dma((ring,))] * 10
        + [dma((wide,))] * 6
        + [dma((chunks,))] * 2
        + [dma((18,))],
        compiler_params=pltpu.CompilerParams(
            collective_id=0, has_side_effects=True, vmem_limit_bytes=60 * 1024 * 1024
        ),
    )(tokens, expert_ids, gate_weights, w_gate, w_up, w_down)


def solution(mesh):
    in_specs = (
        P(("group", "expert"), None),
        P(("group", "expert"), None),
        P(("group", "expert"), None),
        P(("group", "expert"), None, None),
        P(("group", "expert"), None, None),
        P(("group", "expert"), None, None),
    )
    out_specs = P(("group", "expert"), None)
    return jax.shard_map(
        on_device, mesh=mesh, in_specs=in_specs, out_specs=out_specs, check_vma=False
    )
```
